256 devices in a mesh: wide: 64 (over x, z, core), narrow: 4 (over y).
Axes of the slice: x: 4, y: 4, z: 8, core: 2. Of those that a mesh axis runs over, the one named last changes fastest.
Arguments:
- activations: bfloat16 [512, 8192], P('wide', 'narrow'), may hold values from -6 to 6
- up_weight: bfloat16 [8192, 28672], P('narrow', 'wide'), may hold values from -0.0625 to 0.0625
- block_mask: int32 [128, 448], P('narrow', 'wide'), may hold values from 0 to 1, as said below
- out_grad: bfloat16 [512, 28672], P('narrow', 'wide'), may hold values from -6 to 6
Outputs:
- output: bfloat16 [512, 28672], P('narrow', 'wide')
- input_grad: bfloat16 [512, 8192], P('wide', 'narrow')
- weight_grad: bfloat16 [8192, 28672], P('narrow', 'wide')
The draws below stay inside these ranges and needn't reach their ends.
Inputs may be any that keep to these rules, and one draw needn't show every extreme that they name: block_mask holds 0 or 1; the share of kept blocks differs from one block column to another.
All inputs are finite; a program needn't handle non-finite values.
Results may differ from the reference program's by a relative error of at most 0.012.
Values may be sent and summed in bfloat16 or wider, within the bound.
No kernel may reach another device: no remote copies, remote signals or barrier semaphores. Data moves between devices by JAX's collectives and lax.ppermute only.
A program may use at most 64 MiB of HBM per device.

```python
import jax
import jax.numpy as jnp
from jax import lax

D = 8192
FF = 28672
BLOCK = 64
TOKENS = 512
DB = 128
FB = 448


def draw_block_mask(key, part):
    first_key, second_key = jax.random.split(jax.random.fold_in(key, 11))
    keep_share = jax.random.randint(first_key, (1, FB), 10, 91)
    rolled = jax.random.randint(second_key, (DB, FB), 0, 100)
    return (rolled < keep_share).astype(jnp.int32)


def block_levels(key, dims, cuts, least, high):
    def one(axis_at, shards_of):
        heights = jax.random.uniform(jax.random.fold_in(jax.random.fold_in(key, 6), axis_at), (shards_of,), jnp.float32, least / len(cuts), high / len(cuts))
        return jnp.repeat(jnp.exp(heights), dims[axis_at] // shards_of).reshape((-1,) + (1,) * (len(dims) - axis_at - 1))

    gain = one(*cuts[0])
    for cut in cuts[1:]:
        gain = gain * one(*cut)
    return gain


def normal_values(key, shape, width, reach, shards=(), kind=jnp.bfloat16):
    result = width * jax.random.normal(key, shape, jnp.float32)
    if shards:
        result = result * block_levels(key, shape, shards, -0.22, 0.18)
    return jnp.clip(result, -reach, reach).astype(kind)


def setup_inputs(seed: int = 0) -> dict:
    key_of = jax.random.split(jax.random.key(seed), 5)
    activations = normal_values(key_of[0], (TOKENS, D), 1.0, 6.0, ((0, 64), (1, 4)))
    up_weight = normal_values(key_of[1], (D, FF), D ** -0.5, 0.0625, ((0, 4), (1, 64)))
    block_mask = draw_block_mask(jax.random.fold_in(key_of[4], 71), 0)
    out_grad = normal_values(key_of[3], (TOKENS, FF), 1.0, 6.0, ((0, 4), (1, 64)))
    return {"activations": activations, "up_weight": up_weight, "block_mask": block_mask, "out_grad": out_grad}


def apply_mask(weight, blocks):
    rows_b, cols_b = blocks.shape
    shaped = weight.reshape(rows_b, BLOCK, cols_b, BLOCK)
    return (shaped * blocks[:, None, :, None].astype(weight.dtype)).reshape(weight.shape)


def reference(activations, up_weight, block_mask, out_grad):
    masked = apply_mask(up_weight, block_mask)
    output = jnp.dot(activations, masked, preferred_element_type=jnp.float32).astype(jnp.bfloat16)
    input_grad = lax.dot_general(out_grad, masked, (((1,), (1,)), ((), ())), preferred_element_type=jnp.float32).astype(jnp.bfloat16)
    full_grad = lax.dot_general(activations, out_grad, (((0,), (0,)), ((), ())), preferred_element_type=jnp.float32)
    weight_grad = apply_mask(full_grad, block_mask).astype(jnp.bfloat16)
    return (output, input_grad, weight_grad)
```

```python
import jax
import jax.numpy as jnp
from jax import lax
from jax.experimental import pallas as pl
from jax.experimental.pallas import tpu as pltpu
from jax.sharding import Mesh
from jax.sharding import PartitionSpec as P

WIDE = ("x", "z", "core")
BF = jnp.bfloat16
F32 = jnp.float32


def cost(flops, moved):
    return pl.CostEstimate(flops=flops, bytes_accessed=moved, transcendentals=0)


def spread(mask, rows_b, cols):
    cols_b = mask.shape[1]
    side = cols // cols_b
    block = lax.broadcasted_iota(jnp.int32, (cols_b, cols), 0)
    at = lax.broadcasted_iota(jnp.int32, (cols_b, cols), 1)
    first = block * side
    pick = jnp.logical_and(at >= first, at < first + side).astype(F32)
    return jnp.dot(mask.astype(F32), pick, preferred_element_type=F32)


def mask_kernel(w_ref, m_ref, o_ref):
    rows, cols = w_ref.shape
    rows_b = m_ref.shape[0]
    side = rows // rows_b
    wide = spread(m_ref[...], rows_b, cols)
    for i in range(rows_b):
        span = pl.ds(i * side, side)
        o_ref[span, :] = w_ref[span, :] * wide[i : i + 1, :].astype(BF)


def masked_weight(wt, mt):
    return pl.pallas_call(
        mask_kernel,
        out_shape=jax.ShapeDtypeStruct(wt.shape, BF),
        in_specs=[pl.BlockSpec(memory_space=pltpu.VMEM)] * 2,
        out_specs=pl.BlockSpec(memory_space=pltpu.VMEM),
        cost_estimate=cost(wt.size * 2, wt.size * 4),
        name="mask_weight",
    )(wt, mt)


def dgrad_kernel(core_ref, dy_ref, w_ref, keep_ref, send_ref):
    total = lax.dot_general(
        dy_ref[0], w_ref[...], (((0,), (0,)), ((), ())), preferred_element_type=F32
    )
    rows, cols = total.shape
    split = total.reshape(rows // 16, 2, 8, cols)
    low, high = split[:, 0], split[:, 1]
    second = core_ref[0] == 1
    keep_ref[0] = jnp.where(second, high, low).reshape(rows // 2, cols).astype(BF)
    send_ref[0] = jnp.where(second, low, high).reshape(rows // 2, cols).astype(BF)


def dgrad(core, dyg, masked):
    n, hidden, rows = dyg.shape
    cols = masked.shape[1]
    half = jax.ShapeDtypeStruct((n, rows // 2, cols), BF)
    block = pl.BlockSpec((1, rows // 2, cols), lambda i, c: (i, 0, 0))
    return pl.pallas_call(
        dgrad_kernel,
        out_shape=(half, half),
        grid_spec=pltpu.PrefetchScalarGridSpec(
            num_scalar_prefetch=1,
            grid=(n,),
            in_specs=[
                pl.BlockSpec((1, hidden, rows), lambda i, c: (i, 0, 0)),
                pl.BlockSpec((hidden, cols), lambda i, c: (0, 0)),
            ],
            out_specs=(block, block),
        ),
        cost_estimate=cost(2 * n * rows * hidden * cols, 6 << 20),
        name="dgrad",
    )(core, dyg, masked)


def fwd_kernel(core_ref, mine_ref, other_ref, w_ref, out_ref, full_ref):
    mine, other = mine_ref[0].astype(F32), other_ref[0].astype(F32)
    second = core_ref[0] == 1
    low = jnp.where(second, other, mine)
    high = jnp.where(second, mine, other)
    groups, eight, cols = low.shape
    rows = jnp.stack([low, high], axis=1).reshape(groups * 16, cols).astype(BF)
    full_ref[0] = rows
    out_ref[0] = lax.dot_general(
        w_ref[...], rows, (((1,), (1,)), ((), ())), preferred_element_type=F32
    ).astype(BF)


def forward(core, mine, other, masked):
    n, groups, eight, cols = mine.shape
    hidden = masked.shape[0]
    rows = groups * 16
    block = pl.BlockSpec((1, groups, eight, cols), lambda i, c: (i, 0, 0, 0))
    return pl.pallas_call(
        fwd_kernel,
        out_shape=(
            jax.ShapeDtypeStruct((n, hidden, rows), BF),
            jax.ShapeDtypeStruct((n, rows, cols), BF),
        ),
        grid_spec=pltpu.PrefetchScalarGridSpec(
            num_scalar_prefetch=1,
            grid=(n,),
            in_specs=[block, block, pl.BlockSpec((hidden, cols), lambda i, c: (0, 0))],
            out_specs=(
                pl.BlockSpec((1, hidden, rows), lambda i, c: (i, 0, 0)),
                pl.BlockSpec((1, rows, cols), lambda i, c: (i, 0, 0)),
            ),
        ),
        cost_estimate=cost(2 * n * rows * hidden * cols, 6 << 20),
        name="forward",
    )(core, mine, other, masked)


def wgrad_kernel(dy_ref, a_ref, m_ref, o_ref):
    n, hidden, rows = dy_ref.shape
    cols = a_ref.shape[2]
    total = jnp.dot(dy_ref[0], a_ref[0], preferred_element_type=F32)
    for i in range(1, n):
        total += jnp.dot(dy_ref[i], a_ref[i], preferred_element_type=F32)
    rows_b = m_ref.shape[1]
    side = hidden // rows_b
    wide = spread(m_ref[0], rows_b, cols)
    for i in range(rows_b):
        o_ref[i * side : (i + 1) * side, :] = (
            total[i * side : (i + 1) * side] * wide[i : i + 1, :]
        ).astype(BF)


def wgrad(dyg, full, mt):
    n, hidden, rows = dyg.shape
    cols = full.shape[2]
    steps = 4
    tile = cols // steps
    rows_b, cols_b = mt.shape
    parts = jnp.stack(jnp.split(mt, steps, axis=1))
    return pl.pallas_call(
        wgrad_kernel,
        out_shape=jax.ShapeDtypeStruct((hidden, cols), BF),
        grid=(steps,),
        in_specs=[
            pl.BlockSpec((n, hidden, rows), lambda i: (0, 0, 0)),
            pl.BlockSpec((n, rows, tile), lambda i: (0, 0, i)),
            pl.BlockSpec((1, rows_b, cols_b // steps), lambda i: (i, 0, 0)),
        ],
        out_specs=pl.BlockSpec((hidden, tile), lambda i: (0, i)),
        cost_estimate=cost(2 * n * rows * hidden * cols, 6 << 20),
        name="wgrad",
    )(dyg, full, parts)


def exchange(blocks, axis):
    return lax.all_to_all(blocks, axis, split_axis=0, concat_axis=0, tiled=True)


def copies(array, axis):
    return jnp.broadcast_to(array, (lax.axis_size(axis), *array.shape))


def swap(array):
    return lax.ppermute(array, "core", [(0, 1), (1, 0)])


def summed(blocks):
    return blocks.astype(F32).sum(axis=0).astype(BF)


def on_device(activations, up_weight, block_mask, out_grad):
    core = lax.axis_index("core").astype(jnp.int32).reshape(1)
    wt, mt, dyt = up_weight.T, block_mask.T, out_grad.T
    masked = masked_weight(wt, mt)
    dyg = exchange(copies(dyt, "narrow"), "narrow")
    near = exchange(copies(activations, "z"), "z")

    keep, send = dgrad(core, dyg, masked)
    paired = (keep.astype(F32) + swap(send).astype(F32)).astype(BF)
    along_x = summed(exchange(paired, "x"))
    along_z = exchange(along_x.reshape(8, 8, -1), "z")
    input_grad = summed(along_z)

    mine = exchange(copies(near, "x"), "x")
    other = swap(mine)
    partial, full = forward(core, mine, other, masked)
    output = summed(exchange(partial, "narrow")).T
    weight_grad = wgrad(dyg, full, mt).T
    return (output, input_grad, weight_grad)


def solution(mesh):
    torus = Mesh(
        mesh.devices.reshape(4, 8, 2, mesh.shape["narrow"]),
        ("x", "z", "core", "narrow"),
    )
    return jax.shard_map(
        on_device,
        mesh=torus,
        in_specs=(P(WIDE, "narrow"), P("narrow", WIDE), P("narrow", WIDE), P("narrow", WIDE)),
        out_specs=(P("narrow", WIDE), P(WIDE, "narrow"), P("narrow", WIDE)),
        check_vma=False,
    )
```

```python
import jax
import jax.numpy as jnp
from jax import lax
from jax.experimental import pallas as pl
from jax.experimental.pallas import tpu as pltpu
from jax.sharding import Mesh
from jax.sharding import PartitionSpec as P

WIDE = ("x", "z", "core")
BF = jnp.bfloat16
F32 = jnp.float32
VMEM = pl.BlockSpec(memory_space=pltpu.VMEM)
SMEM = pl.BlockSpec(memory_space=pltpu.SMEM)


def cost(flops, moved):
    return pl.CostEstimate(flops=flops, bytes_accessed=moved, transcendentals=0)


def grant(mib):
    return pltpu.CompilerParams(vmem_limit_bytes=mib << 20)


def shaped(*dims, kind=BF):
    return jax.ShapeDtypeStruct(dims, kind)


def mask_kernel(w_ref, m_ref, o_ref, wide_ref):
    rows, cols = w_ref.shape
    rows_b, cols_b = m_ref.shape
    side = cols // cols_b
    block = lax.broadcasted_iota(jnp.int32, (cols_b, cols), 0)
    at = lax.broadcasted_iota(jnp.int32, (cols_b, cols), 1)
    first = block * side
    pick = jnp.logical_and(at >= first, at < first + side).astype(F32)
    wide = jnp.dot(m_ref[...].astype(F32), pick, preferred_element_type=F32)
    wide_ref[...] = wide
    side = rows // rows_b
    for i in range(rows_b):
        span = pl.ds(i * side, side)
        o_ref[span, :] = w_ref[span, :] * wide[i : i + 1, :].astype(BF)


def masked_weight(wt, mt):
    return pl.pallas_call(
        mask_kernel,
        out_shape=(shaped(*wt.shape), shaped(mt.shape[0], wt.shape[1], kind=F32)),
        in_specs=[VMEM] * 2,
        out_specs=(VMEM, VMEM),
        cost_estimate=cost(wt.size * 2, wt.size * 4),
        compiler_params=grant(8),
        name="mask_weight",
    )(wt, mt)


def own_first(core, tokens, back=False):
    old = lax.broadcasted_iota(jnp.int32, (tokens, tokens), 1 if back else 0)
    new = lax.broadcasted_iota(jnp.int32, (tokens, tokens), 0 if back else 1)
    half = tokens // 2
    other = (new >= half).astype(jnp.int32)
    within = new - other * half
    group = jnp.right_shift(within, 3)
    src = group * 16 + jnp.bitwise_xor(other, core) * 8 + (within - group * 8)
    return (src == old).astype(BF)


def dgrad_kernel(at_ref, d0, d1, d2, d3, w_ref, keep_ref, send_ref, dy_ref):
    x, y, core = at_ref[0], at_ref[1], at_ref[2]
    tokens = d0.shape[1]
    half = tokens // 2
    order = own_first(core, tokens)
    for k, d in enumerate((d0, d1, d2, d3)):
        rel = lax.rem(y + k - x + 4, 4)
        lanes = jnp.dot(d[...], order, preferred_element_type=F32).astype(BF)
        dy_ref[:, pl.ds(pl.multiple_of(rel * tokens, tokens), tokens)] = lanes
        total = lax.dot_general(
            lanes, w_ref[...], (((0,), (0,)), ((), ())), preferred_element_type=F32
        ).astype(BF)
        keep_ref[rel] = total[:half]
        send_ref[rel] = total[half:]


def dgrad(at, blocks, masked):
    hidden, tokens = blocks[0].shape
    cols = masked.shape[1]
    half = shaped(4, tokens // 2, cols)
    return pl.pallas_call(
        dgrad_kernel,
        out_shape=(half, half, shaped(hidden, 4 * tokens)),
        in_specs=[SMEM] + [VMEM] * 5,
        out_specs=(VMEM,) * 3,
        cost_estimate=cost(8 * tokens * hidden * cols, 4 << 20),
        compiler_params=grant(16),
        name="dgrad",
    )(at, *blocks, masked)


def fwd_kernel(at_ref, *refs):
    mine, other = refs[:5], refs[5:10]
    w_ref, o0, o1, o2, o3, full_ref, acc_ref = refs[10:]
    x, y = at_ref[0], at_ref[1]
    half = mine[0].shape[0]
    quarter = half // 2
    for h, group in enumerate((mine, other)):
        for k in range(3):
            full_ref[pl.ds((0, 2, 6)[k] * half + h * half, half), :] = group[k][...]
        full_ref[pl.ds(4 * half + h * half, quarter), :] = group[3][...]
        full_ref[pl.ds(4 * half + h * half + quarter, quarter), :] = group[4][...]
    acc_ref[...] = lax.dot_general(
        w_ref[...], full_ref[...], (((1,), (1,)), ((), ())), preferred_element_type=F32
    ).astype(BF)
    tokens = 2 * half
    for k, out in enumerate((o0, o1, o2, o3)):
        rel = lax.rem(y + k - x + 4, 4)
        out[...] = acc_ref[:, pl.ds(pl.multiple_of(rel * tokens, tokens), tokens)]


def forward(at, mine, other, masked):
    half = mine[0].shape[0]
    hidden, cols = masked.shape
    out = shaped(hidden, 2 * half)
    return pl.pallas_call(
        fwd_kernel,
        out_shape=(out,) * 4 + (shaped(8 * half, cols),),
        in_specs=[SMEM] + [VMEM] * 11,
        out_specs=(VMEM,) * 5,
        scratch_shapes=[pltpu.VMEM((hidden, 8 * half), BF)],
        cost_estimate=cost(16 * half * hidden * cols, 6 << 20),
        compiler_params=grant(16),
        name="forward",
    )(at, *mine, *other, masked)


def wgrad_kernel(dy_ref, a_ref, wide_ref, o_ref):
    total = jnp.dot(dy_ref[...], a_ref[...], preferred_element_type=F32)
    rows_b = wide_ref.shape[0]
    side = total.shape[0] // rows_b
    for i in range(rows_b):
        span = slice(i * side, (i + 1) * side)
        o_ref[span, :] = (total[span] * wide_ref[i : i + 1, :]).astype(BF)


def wgrad(dy, full, wide):
    hidden, rows = dy.shape
    cols = full.shape[1]
    steps = 4
    tile = cols // steps
    return pl.pallas_call(
        wgrad_kernel,
        out_shape=shaped(hidden, cols),
        grid=(steps,),
        in_specs=[
            pl.BlockSpec((hidden, rows), lambda i: (0, 0)),
            pl.BlockSpec((rows, tile), lambda i: (0, i)),
            pl.BlockSpec((wide.shape[0], tile), lambda i: (0, i)),
        ],
        out_specs=pl.BlockSpec((hidden, tile), lambda i: (0, i)),
        cost_estimate=cost(2 * rows * hidden * cols, 6 << 20),
        compiler_params=grant(14),
        name="wgrad",
    )(dy, full, wide)


def finish_kernel(at_ref, r0, r1, r2, r3, o_ref):
    total = (r0[...].astype(F32) + r1[...].astype(F32)) + (
        r2[...].astype(F32) + r3[...].astype(F32)
    )
    back = own_first(at_ref[2], r0.shape[1], back=True)
    o_ref[...] = jnp.dot(total.astype(BF), back, preferred_element_type=F32).astype(BF)


def finish(at, parts):
    return pl.pallas_call(
        finish_kernel,
        out_shape=shaped(*parts[0].shape),
        in_specs=[SMEM] + [VMEM] * 4,
        out_specs=VMEM,
        cost_estimate=cost(parts[0].size * 256, 1 << 20),
        compiler_params=grant(6),
        name="finish",
    )(at, *parts)


def exchange(blocks, axis):
    return lax.all_to_all(blocks, axis, split_axis=0, concat_axis=0, tiled=True)


def copies(array, axis):
    return jnp.broadcast_to(array, (lax.axis_size(axis), *array.shape))


def to(array, axis, step):
    n = lax.axis_size(axis)
    return lax.ppermute(array, axis, [(i, (i + step) % n) for i in range(n)])


def added(*terms):
    return sum(t.astype(F32) for t in terms).astype(BF)


def on_device(activations, up_weight, block_mask, out_grad):
    at = jnp.stack([lax.axis_index(n).astype(jnp.int32) for n in ("x", "narrow", "core")])
    wt, mt, dyt = up_weight.T, block_mask.T, out_grad.T
    masked, wide = masked_weight(wt, mt)

    blocks = [to(dyt, "narrow", -1), to(dyt, "narrow", 1)]
    blocks = (dyt, blocks[0], to(dyt, "narrow", 2), blocks[1])
    near = exchange(copies(activations, "z"), "z").reshape(-1, activations.shape[1])

    keep, send, dy = dgrad(at, blocks, masked)
    got = to(send, "core", 1)
    half = keep.shape[1] // 2
    ahead = to(added(keep[2, :half], got[2, :half]), "x", 1)
    behind = to(added(keep[2, half:], got[2, half:]), "x", -1)
    none = jnp.zeros_like(ahead)
    right = added(keep[1], got[1], jnp.concatenate([ahead, none]))
    left = added(keep[3], got[3], jnp.concatenate([none, behind]))
    along_x = added(keep[0], got[0], to(right, "x", 1), to(left, "x", -1))
    along_z = exchange(along_x.reshape(8, 8, -1), "z")
    input_grad = along_z.astype(F32).sum(axis=0).astype(BF)

    after, before = to(near, "x", -1), to(near, "x", 1)
    far_low, far_high = to(before[:half], "x", 1), to(after[half:], "x", -1)
    mine = (near, after, before, far_low, far_high)
    other = tuple(to(m, "core", 1) for m in mine)
    o0, o1, o2, o3, full = forward(at, mine, other, masked)
    parts = (o0, to(o1, "narrow", 1), to(o2, "narrow", 2), to(o3, "narrow", -1))
    output = finish(at, parts).T
    weight_grad = wgrad(dy, full, wide).T
    return (output, input_grad, weight_grad)


def solution(mesh):
    torus = Mesh(
        mesh.devices.reshape(4, 8, 2, mesh.shape["narrow"]),
        ("x", "z", "core", "narrow"),
    )
    return jax.shard_map(
        on_device,
        mesh=torus,
        in_specs=(P(WIDE, "narrow"), P("narrow", WIDE), P("narrow", WIDE), P("narrow", WIDE)),
        out_specs=(P("narrow", WIDE), P(WIDE, "narrow"), P("narrow", WIDE)),
        check_vma=False,
    )
```

```python
import jax
import jax.numpy as jnp
from jax import lax
from jax.experimental import pallas as pl
from jax.experimental.pallas import tpu as pltpu
from jax.sharding import Mesh
from jax.sharding import PartitionSpec as P

WIDE = ("x", "z", "core")
BF = jnp.bfloat16
F32 = jnp.float32
VMEM = pl.BlockSpec(memory_space=pltpu.VMEM)
HBM = pl.BlockSpec(memory_space=pltpu.HBM)
SMEM = pl.BlockSpec(memory_space=pltpu.SMEM)


def cost(flops, moved):
    return pl.CostEstimate(flops=flops, bytes_accessed=moved, transcendentals=0)


def grant(mib):
    return pltpu.CompilerParams(vmem_limit_bytes=mib << 20)


def in_hbm(array):
    return pltpu.with_memory_space_constraint(array, pltpu.HBM)


def shaped(*dims, kind=BF):
    return jax.ShapeDtypeStruct(dims, kind)


def spread(mask, cols):
    cols_b = mask.shape[1]
    side = cols // cols_b
    block = lax.broadcasted_iota(jnp.int32, (cols_b, cols), 0)
    at = lax.broadcasted_iota(jnp.int32, (cols_b, cols), 1)
    first = block * side
    pick = jnp.logical_and(at >= first, at < first + side).astype(F32)
    return jnp.dot(mask.astype(F32), pick, preferred_element_type=F32)


def own_first(core, tokens):
    new = lax.broadcasted_iota(jnp.int32, (tokens, tokens), 0)
    old = lax.broadcasted_iota(jnp.int32, (tokens, tokens), 1)
    half = tokens // 2
    other = (new >= half).astype(jnp.int32)
    within = new - other * half
    group = jnp.right_shift(within, 3)
    src = group * 16 + jnp.bitwise_xor(other, core) * 8 + (within - group * 8)
    return (src == old).astype(BF)


def dgrad_kernel(at_ref, m_ref, d0, d1, d2, d3, w_hbm, keep_ref, send_ref, dy_ref, masked_ref, wide_ref, d_ref, w_ref, d_sems, sems):
    x, y, core = at_ref[0], at_ref[1], at_ref[2]
    hidden, tokens = d0.shape
    cols = w_ref.shape[1]
    loads = [
        pltpu.make_async_copy(d, d_ref.at[k], d_sems.at[k]) for k, d in enumerate((d0, d1, d2, d3))
    ]
    for load in loads:
        load.start()
    rows_b = m_ref.shape[0]
    side = hidden // rows_b

    def fetch(i):
        span = pl.ds(i * side, side)
        return pltpu.make_async_copy(w_hbm.at[span], w_ref.at[span], sems.at[i])

    for i in range(rows_b):
        fetch(i).start()
    half = tokens // 2
    order = own_first(core, tokens)
    wide = spread(m_ref[...], cols)
    wide_ref[...] = wide
    for k, load in enumerate(loads):
        block = lax.rem(y + k, 4)
        load.wait()
        rows = lax.dot_general(
            order, d_ref[k], (((1,), (1,)), ((), ())), preferred_element_type=F32
        ).astype(BF)
        dy_ref[pl.ds(pl.multiple_of(block * half, half), half), :] = rows[:half]
        dy_ref[pl.ds(pl.multiple_of((block + 4) * half, half), half), :] = rows[half:]
    for i in range(rows_b):
        fetch(i).wait()
        span = pl.ds(i * side, side)
        masked_ref[span, :] = w_ref[span, :] * wide[i : i + 1, :].astype(BF)
    steps = 4
    tile = cols // steps
    for j in range(steps):
        span = pl.ds(j * tile, tile)
        total = jnp.dot(dy_ref[...], masked_ref[:, span], preferred_element_type=F32).astype(BF)
        for b in range(4):
            rel = lax.rem(b - x + 4, 4)
            keep_ref[rel, :, span] = total[b * half : (b + 1) * half]
            send_ref[rel, :, span] = total[(b + 4) * half : (b + 5) * half]


def dgrad(at, blocks, mt, wt):
    hidden, tokens = blocks[0].shape
    cols = wt.shape[1]
    half = shaped(4, tokens // 2, cols)
    return pl.pallas_call(
        dgrad_kernel,
        out_shape=(
            half,
            half,
            shaped(4 * tokens, hidden),
            shaped(hidden, cols),
            shaped(mt.shape[0], cols, kind=F32),
        ),
        in_specs=[SMEM, VMEM] + [HBM] * 5,
        out_specs=(VMEM,) * 5,
        scratch_shapes=[
            pltpu.VMEM((4, hidden, tokens), BF),
            pltpu.VMEM((hidden, cols), BF),
            pltpu.SemaphoreType.DMA((4,)),
            pltpu.SemaphoreType.DMA((mt.shape[0],)),
        ],
        cost_estimate=cost(8 * tokens * hidden * cols, 4 << 20),
        compiler_params=grant(20),
        name="dgrad",
    )(at, mt, *blocks, wt)


def fwd_kernel(at_ref, mine_ref, other_ref, w_ref, o0, o1, o2, o3, sum_ref, acc_ref):
    step = pl.program_id(0)
    rows = mine_ref.shape[0]

    @pl.when(step == 0)
    def _():
        sum_ref[...] = jnp.zeros_like(sum_ref)

    for h, ref in enumerate((mine_ref, other_ref)):
        sum_ref[:, h * rows : (h + 1) * rows] += lax.dot_general(
            w_ref[...], ref[...], (((1,), (1,)), ((), ())), preferred_element_type=F32
        )

    @pl.when(step == pl.num_programs(0) - 1)
    def _():
        y = at_ref[1]
        half = rows // 4
        tokens = 2 * half
        for b in range(4):
            own = sum_ref[:, b * half : (b + 1) * half]
            far = sum_ref[:, rows + b * half : rows + (b + 1) * half]
            acc_ref[:, b * tokens : (b + 1) * tokens] = jnp.concatenate([own, far], axis=1).astype(BF)
        for k, out in enumerate((o0, o1, o2, o3)):
            block = lax.rem(y + k, 4)
            out[...] = acc_ref[:, pl.ds(pl.multiple_of(block * tokens, tokens), tokens)]


def forward(at, mine, other, masked):
    rows, cols = mine.shape
    hidden = masked.shape[0]
    out = shaped(hidden, rows // 2)
    steps = 4
    tile = cols // steps
    tokens = pl.BlockSpec((rows, tile), lambda i: (0, i))
    whole = pl.BlockSpec((hidden, rows // 2), lambda i: (0, 0))
    return pl.pallas_call(
        fwd_kernel,
        out_shape=(out,) * 4,
        grid=(steps,),
        in_specs=[SMEM, tokens, tokens, pl.BlockSpec((hidden, tile), lambda i: (0, i))],
        out_specs=(whole,) * 4,
        scratch_shapes=[pltpu.VMEM((hidden, 2 * rows), F32), pltpu.VMEM((hidden, 2 * rows), BF)],
        cost_estimate=cost(4 * rows * hidden * cols, 6 << 20),
        compiler_params=grant(14),
        name="forward",
    )(at, mine, other, masked)


def wgrad_kernel(dy_ref, mine_ref, other_ref, wide_ref, o_ref, dyt_ref):
    @pl.when(pl.program_id(0) == 0)
    def _():
        dyt_ref[...] = dy_ref[...].T

    rows = mine_ref.shape[0]
    total = jnp.dot(dyt_ref[:, :rows], mine_ref[...], preferred_element_type=F32)
    total += jnp.dot(dyt_ref[:, rows:], other_ref[...], preferred_element_type=F32)
    rows_b = wide_ref.shape[0]
    side = total.shape[0] // rows_b
    for i in range(rows_b):
        span = slice(i * side, (i + 1) * side)
        o_ref[span, :] = (total[span] * wide_ref[i : i + 1, :]).astype(BF)


def wgrad(dy, mine, other, wide):
    rows, hidden = dy.shape
    cols = mine.shape[1]
    steps = 4
    tile = cols // steps
    return pl.pallas_call(
        wgrad_kernel,
        out_shape=shaped(hidden, cols),
        grid=(steps,),
        in_specs=[
            pl.BlockSpec((rows, hidden), lambda i: (0, 0)),
            pl.BlockSpec((rows // 2, tile), lambda i: (0, i)),
            pl.BlockSpec((rows // 2, tile), lambda i: (0, i)),
            pl.BlockSpec((wide.shape[0], tile), lambda i: (0, i)),
        ],
        out_specs=pl.BlockSpec((hidden, tile), lambda i: (0, i)),
        scratch_shapes=[pltpu.VMEM((hidden, rows), BF)],
        cost_estimate=cost(2 * rows * hidden * cols, 6 << 20),
        compiler_params=grant(14),
        name="wgrad",
    )(dy, mine, other, wide)


def finish_kernel(at_ref, r0, r1, r2, r3, o_ref):
    total = (r0[...].astype(F32) + r1[...].astype(F32)) + (
        r2[...].astype(F32) + r3[...].astype(F32)
    )
    back = own_first(at_ref[2], r0.shape[1])
    o_ref[...] = jnp.dot(total.astype(BF), back, preferred_element_type=F32).astype(BF)


def finish(at, parts):
    return pl.pallas_call(
        finish_kernel,
        out_shape=shaped(*parts[0].shape),
        in_specs=[SMEM] + [VMEM] * 4,
        out_specs=VMEM,
        cost_estimate=cost(parts[0].size * 256, 1 << 20),
        compiler_params=grant(6),
        name="finish",
    )(at, *parts)


def exchange(blocks, axis):
    return lax.all_to_all(blocks, axis, split_axis=0, concat_axis=0, tiled=True)


def copies(array, axis):
    return jnp.broadcast_to(array, (lax.psum(1, axis), *array.shape))


def to(array, axis, step):
    n = lax.axis_size(axis)
    return lax.ppermute(array, axis, [(i, (i + step) % n) for i in range(n)])


def added(*terms):
    return sum(t.astype(F32) for t in terms).astype(BF)


def on_device(activations, up_weight, block_mask, out_grad):
    at = jnp.stack([lax.axis_index(n).astype(jnp.int32) for n in ("x", "narrow", "core")])
    wt, mt, dyt = up_weight.T, block_mask.T, out_grad.T

    blocks = (dyt, to(dyt, "narrow", -1), to(dyt, "narrow", 2), to(dyt, "narrow", 1))
    mine = exchange(copies(activations, ("x", "z")), ("x", "z")).reshape(-1, activations.shape[1])

    keep, send, dy, masked, wide = dgrad(at, [in_hbm(b) for b in blocks], mt, in_hbm(wt))
    got = to(send, "core", 1)
    half = keep.shape[1] // 2
    ahead = to(added(keep[2, :half], got[2, :half]), "x", 1)
    behind = to(added(keep[2, half:], got[2, half:]), "x", -1)
    none = jnp.zeros_like(ahead)
    right = added(keep[1], got[1], jnp.concatenate([ahead, none]))
    left = added(keep[3], got[3], jnp.concatenate([none, behind]))
    along_x = added(keep[0], got[0], to(right, "x", 1), to(left, "x", -1))
    along_z = exchange(along_x.reshape(8, 8, -1), "z")
    input_grad = along_z.astype(F32).sum(axis=0).astype(BF)

    other = to(mine, "core", 1)
    o0, o1, o2, o3 = forward(at, mine, other, masked)
    parts = (o0, to(o1, "narrow", 1), to(o2, "narrow", 2), to(o3, "narrow", -1))
    output = finish(at, parts).T
    weight_grad = wgrad(dy, mine, other, wide).T
    return (output, input_grad, weight_grad)


def solution(mesh):
    torus = Mesh(
        mesh.devices.reshape(4, 8, 2, mesh.shape["narrow"]),
        ("x", "z", "core", "narrow"),
    )
    return jax.shard_map(
        on_device,
        mesh=torus,
        in_specs=(P(WIDE, "narrow"), P("narrow", WIDE), P("narrow", WIDE), P("narrow", WIDE)),
        out_specs=(P("narrow", WIDE), P(WIDE, "narrow"), P("narrow", WIDE)),
        check_vma=False,
    )
```

```python
import functools

import jax
import jax.numpy as jnp
from jax import lax
from jax.experimental import pallas as pl
from jax.experimental.pallas import tpu as pltpu
from jax.sharding import Mesh
from jax.sharding import PartitionSpec as P

WIDE = ("x", "z", "core")
BF = jnp.bfloat16
F32 = jnp.float32
VMEM = pl.BlockSpec(memory_space=pltpu.VMEM)
HBM = pl.BlockSpec(memory_space=pltpu.HBM)
SMEM = pl.BlockSpec(memory_space=pltpu.SMEM)


def cost(flops, moved):
    return pl.CostEstimate(flops=flops, bytes_accessed=moved, transcendentals=0)


def grant(mib):
    return pltpu.CompilerParams(vmem_limit_bytes=mib << 20)


def in_hbm(array):
    return pltpu.with_memory_space_constraint(array, pltpu.HBM)


def shaped(*dims, kind=BF):
    return jax.ShapeDtypeStruct(dims, kind)


def spread(mask, start, tile, cols):
    cols_b = mask.shape[1]
    side = cols // cols_b
    block = lax.broadcasted_iota(jnp.int32, (cols_b, tile), 0)
    at = lax.broadcasted_iota(jnp.int32, (cols_b, tile), 1) + start
    first = block * side
    pick = jnp.logical_and(at >= first, at < first + side).astype(F32)
    return jnp.dot(mask.astype(F32), pick, preferred_element_type=F32)


def own_first(core, z, tokens):
    new = lax.broadcasted_iota(jnp.int32, (tokens, tokens), 0)
    old = lax.broadcasted_iota(jnp.int32, (tokens, tokens), 1)
    half = tokens // 2
    other = (new >= half).astype(jnp.int32)
    within = new - other * half
    group = jnp.right_shift(within, 3)
    row = within - group * 8
    low = jnp.right_shift(group, 2)
    mid = jnp.bitwise_and(group, 2)
    high = jnp.bitwise_and(group, 1) * 4
    src = jnp.bitwise_xor(low + mid + high, z) * 16 + jnp.bitwise_xor(other, core) * 8 + row
    return (src == old).astype(BF)


def mask_kernel(m_hbm, w_hbm, masked_ref, m_ref, w_ref, m_sem, sems):
    rows, cols = w_ref.shape
    rows_b = m_ref.shape[0]
    side = rows // rows_b
    spans = [pl.ds(i * side, side) for i in range(rows_b)]
    first = pltpu.make_async_copy(m_hbm, m_ref, m_sem)
    first.start()
    loads = [
        pltpu.make_async_copy(w_hbm.at[span], w_ref.at[span], sems.at[i])
        for i, span in enumerate(spans)
    ]
    for load in loads:
        load.start()
    first.wait()
    wide = spread(m_ref[...], 0, cols, cols)
    for i, span in enumerate(spans):
        loads[i].wait()
        masked_ref[span, :] = w_ref[span, :] * wide[i : i + 1, :].astype(BF)


def masked_weight(mt, wt):
    hidden, cols = wt.shape
    return pl.pallas_call(
        mask_kernel,
        out_shape=shaped(hidden, cols),
        in_specs=[HBM, HBM],
        out_specs=VMEM,
        scratch_shapes=[
            pltpu.VMEM(mt.shape, jnp.int32),
            pltpu.VMEM((hidden, cols), BF),
            pltpu.SemaphoreType.DMA,
            pltpu.SemaphoreType.DMA((mt.shape[0],)),
        ],
        cost_estimate=cost(2 * hidden * cols, 4 << 20),
        compiler_params=grant(10),
        name="mask_weight",
    )(mt, wt)


def dgrad_kernel(at_ref, d0, d1, d2, d3, w_ref, keep_ref, send_ref, dy_ref):
    x, y, core, z = (at_ref[i] for i in range(4))
    tokens = d0.shape[1]
    cols = w_ref.shape[1]
    half = tokens // 2
    order = own_first(core, z, tokens)
    for k, d in enumerate((d0, d1, d2, d3)):
        rel = lax.rem(y + k - x + 4, 4)
        dy_ref[pl.ds(pl.multiple_of(rel * tokens, tokens), tokens), :] = lax.dot_general(
            order, d[...], (((1,), (1,)), ((), ())), preferred_element_type=F32
        ).astype(BF)
    steps = 4
    tile = cols // steps
    for j in range(steps):
        span = pl.ds(j * tile, tile)
        total = jnp.dot(dy_ref[...], w_ref[:, span], preferred_element_type=F32).astype(BF)
        for p in range(4):
            first = p * tokens
            keep_ref[p, :, span] = total[first : first + half]
            send_ref[p, :, span] = total[first + half : first + tokens]


def dgrad(at, blocks, masked):
    hidden, tokens = blocks[0].shape
    cols = masked.shape[1]
    half = shaped(4, tokens // 2, cols)
    return pl.pallas_call(
        dgrad_kernel,
        out_shape=(half, half, shaped(4 * tokens, hidden)),
        in_specs=[SMEM] + [VMEM] * 5,
        out_specs=(VMEM,) * 3,
        cost_estimate=cost(8 * tokens * hidden * cols, 4 << 20),
        compiler_params=grant(12),
        name="dgrad",
    )(at, *blocks, masked)


def fwd_kernel(at_ref, *refs):
    mine, other = refs[:4], refs[4:8]
    w_ref, o0, o1, o2, o3, full_ref, acc_ref = refs[8:]
    x, y = at_ref[0], at_ref[1]
    half = mine[0].shape[0]
    tokens = 2 * half
    for p in range(4):
        full_ref[p * tokens : p * tokens + half, :] = mine[p][...]
        full_ref[p * tokens + half : (p + 1) * tokens, :] = other[p][...]
    acc_ref[...] = lax.dot_general(
        w_ref[...], full_ref[...], (((1,), (1,)), ((), ())), preferred_element_type=F32
    ).astype(BF)
    for k, out in enumerate((o0, o1, o2, o3)):
        rel = lax.rem(y + k - x + 4, 4)
        out[...] = acc_ref[:, pl.ds(pl.multiple_of(rel * tokens, tokens), tokens)]


def forward(at, mine, other, masked):
    half, cols = mine[0].shape
    hidden = masked.shape[0]
    out = shaped(hidden, 2 * half)
    return pl.pallas_call(
        fwd_kernel,
        out_shape=(out,) * 4 + (shaped(8 * half, cols),),
        in_specs=[SMEM] + [VMEM] * 9,
        out_specs=(VMEM,) * 5,
        scratch_shapes=[pltpu.VMEM((hidden, 8 * half), BF)],
        cost_estimate=cost(16 * half * hidden * cols, 6 << 20),
        compiler_params=grant(14),
        name="forward",
    )(at, *mine, *other, masked)


def wgrad_kernel(cols, dy_ref, a_ref, m_ref, o_ref, dyt_ref):
    step = pl.program_id(0)

    @pl.when(step == 0)
    def _():
        dyt_ref[...] = dy_ref[...].T

    total = jnp.dot(dyt_ref[...], a_ref[...], preferred_element_type=F32)
    rows_b = m_ref.shape[0]
    tile = a_ref.shape[1]
    wide = spread(m_ref[...], step * tile, tile, cols)
    side = total.shape[0] // rows_b
    for i in range(rows_b):
        span = slice(i * side, (i + 1) * side)
        o_ref[span, :] = (total[span] * wide[i : i + 1, :]).astype(BF)


def wgrad(dy, full, mt):
    rows, hidden = dy.shape
    cols = full.shape[1]
    steps = 4
    tile = cols // steps
    return pl.pallas_call(
        functools.partial(wgrad_kernel, cols),
        out_shape=shaped(hidden, cols),
        grid=(steps,),
        in_specs=[
            pl.BlockSpec((rows, hidden), lambda i: (0, 0)),
            pl.BlockSpec((rows, tile), lambda i: (0, i)),
            pl.BlockSpec(mt.shape, lambda i: (0, 0)),
        ],
        out_specs=pl.BlockSpec((hidden, tile), lambda i: (0, i)),
        scratch_shapes=[pltpu.VMEM((hidden, rows), BF)],
        cost_estimate=cost(2 * rows * hidden * cols, 6 << 20),
        compiler_params=grant(14),
        name="wgrad",
    )(dy, full, mt)


def finish_kernel(at_ref, r0, r1, r2, r3, o_ref):
    total = (r0[...].astype(F32) + r1[...].astype(F32)) + (
        r2[...].astype(F32) + r3[...].astype(F32)
    )
    back = own_first(at_ref[2], at_ref[3], r0.shape[1])
    o_ref[...] = jnp.dot(total.astype(BF), back, preferred_element_type=F32).astype(BF)


def finish(at, parts):
    return pl.pallas_call(
        finish_kernel,
        out_shape=shaped(*parts[0].shape),
        in_specs=[SMEM] + [VMEM] * 4,
        out_specs=VMEM,
        cost_estimate=cost(parts[0].size * 256, 1 << 20),
        compiler_params=grant(6),
        name="finish",
    )(at, *parts)


def to(array, axis, step):
    n = lax.axis_size(axis)
    return lax.ppermute(array, axis, [(i, (i + step) % n) for i in range(n)])


def with_partner(array, bit):
    return jnp.concatenate([array, across(array, bit)])


def across(array, bit):
    return lax.ppermute(array, "z", [(i, i ^ bit) for i in range(lax.axis_size("z"))])


def halved(*terms):
    half = terms[0].shape[0] // 2
    return added(*(t[:half] for t in terms)), added(*(t[half:] for t in terms))


def added(*terms):
    return sum(t.astype(F32) for t in terms).astype(BF)


def on_device(activations, up_weight, block_mask, out_grad):
    at = jnp.stack([lax.axis_index(n).astype(jnp.int32) for n in ("x", "narrow", "core", "z")])
    wt, mt, dyt = up_weight.T, block_mask.T, out_grad.T

    blocks = (dyt, to(dyt, "narrow", -1), to(dyt, "narrow", 2), to(dyt, "narrow", 1))
    masked = masked_weight(in_hbm(mt), in_hbm(wt))
    near = with_partner(activations, 4)
    keep, send, dy = dgrad(at, blocks, masked)
    got = to(send, "core", 1)
    near = with_partner(near, 2)
    near = with_partner(near, 1)
    second, first = added(keep[2], got[2]), added(keep[1], got[1])
    behind = to(second, "x", -1)
    direct = to(first, "x", 1)
    third = added(keep[3], got[3], behind)
    relayed = to(third, "x", -1)
    own, away = halved(keep[0], got[0], direct, relayed)
    came = across(away, 1)
    own, away = halved(own, came)
    came = across(away, 2)
    own, away = halved(own, came)
    came = across(away, 4)
    input_grad = added(own, came)

    before = to(near, "x", 1)
    after = to(near, "x", -1)
    far = to(before, "x", 1)
    mine = (near, after, far, before)
    other = tuple(to(m, "core", 1) for m in mine)
    o0, o1, o2, o3, full = forward(at, mine, other, masked)
    parts = (o0, to(o1, "narrow", 1), to(o2, "narrow", 2), to(o3, "narrow", -1))
    output = finish(at, parts).T
    weight_grad = wgrad(dy, full, mt).T
    return (output, input_grad, weight_grad)


def solution(mesh):
    torus = Mesh(
        mesh.devices.reshape(4, 8, 2, mesh.shape["narrow"]),
        ("x", "z", "core", "narrow"),
    )
    return jax.shard_map(
        on_device,
        mesh=torus,
        in_specs=(P(WIDE, "narrow"), P("narrow", WIDE), P("narrow", WIDE), P("narrow", WIDE)),
        out_specs=(P("narrow", WIDE), P(WIDE, "narrow"), P("narrow", WIDE)),
        check_vma=False,
    )
```

```python
import jax
import jax.numpy as jnp
from jax import lax
from jax.experimental import pallas as pl
from jax.experimental.pallas import tpu as pltpu
from jax.sharding import Mesh
from jax.sharding import PartitionSpec as P

WIDE = ("x", "z", "core")
STEPS = (3, -1, 1)
BF = jnp.bfloat16
F32 = jnp.float32
VMEM = pl.BlockSpec(memory_space=pltpu.VMEM)
HBM = pl.BlockSpec(memory_space=pltpu.HBM)
SMEM = pl.BlockSpec(memory_space=pltpu.SMEM)


def cost(flops, moved):
    return pl.CostEstimate(flops=flops, bytes_accessed=moved, transcendentals=0)


def grant(mib):
    return pltpu.CompilerParams(vmem_limit_bytes=mib << 20)


def in_hbm(array):
    return pltpu.with_memory_space_constraint(array, pltpu.HBM)


def shaped(*dims, kind=BF):
    return jax.ShapeDtypeStruct(dims, kind)


def spread(mask, cols):
    cols_b = mask.shape[1]
    side = cols // cols_b
    block = lax.broadcasted_iota(jnp.int32, (cols_b, cols), 0)
    at = lax.broadcasted_iota(jnp.int32, (cols_b, cols), 1)
    first = block * side
    pick = jnp.logical_and(at >= first, at < first + side).astype(F32)
    return jnp.dot(mask.astype(F32), pick, preferred_element_type=F32)


def own_first(core, z, tokens):
    new = lax.broadcasted_iota(jnp.int32, (tokens, tokens), 0)
    old = lax.broadcasted_iota(jnp.int32, (tokens, tokens), 1)
    half = tokens // 2
    other = (new >= half).astype(jnp.int32)
    within = new - other * half
    group = jnp.right_shift(within, 3)
    row = within - group * 8
    at = jnp.zeros_like(group) + z
    for bit, step in zip((2, 1, 0), reversed(STEPS)):
        moved = jnp.bitwise_and(jnp.right_shift(group, bit), 1) * step
        at = at + moved * (1 - 2 * jnp.bitwise_and(at, 1))
    src = jnp.bitwise_and(at, 7) * 16 + jnp.bitwise_xor(other, core) * 8 + row
    return (src == old).astype(BF)


def mask_kernel(m_hbm, w_hbm, masked_ref, m_ref, w_ref, m_sem, sems):
    rows, cols = w_ref.shape
    rows_b = m_ref.shape[0]
    side = rows // rows_b
    spans = [pl.ds(i * side, side) for i in range(rows_b)]
    first = pltpu.make_async_copy(m_hbm, m_ref, m_sem)
    first.start()
    loads = [
        pltpu.make_async_copy(w_hbm.at[span], w_ref.at[span], sems.at[i])
        for i, span in enumerate(spans)
    ]
    for load in loads:
        load.start()
    first.wait()
    wide = spread(m_ref[...], cols)
    for i, span in enumerate(spans):
        loads[i].wait()
        masked_ref[span, :] = w_ref[span, :] * wide[i : i + 1, :].astype(BF)


def masked_weight(mt, wt):
    hidden, cols = wt.shape
    return pl.pallas_call(
        mask_kernel,
        out_shape=shaped(hidden, cols),
        in_specs=[HBM, HBM],
        out_specs=VMEM,
        scratch_shapes=[
            pltpu.VMEM(mt.shape, jnp.int32),
            pltpu.VMEM((hidden, cols), BF),
            pltpu.SemaphoreType.DMA,
            pltpu.SemaphoreType.DMA((mt.shape[0],)),
        ],
        cost_estimate=cost(2 * hidden * cols, 4 << 20),
        compiler_params=grant(10),
        name="mask_weight",
    )(mt, wt)


def dgrad_kernel(at_ref, d0, d1, d2, d3, w_ref, keep_ref, send_ref, dy_ref):
    x, y, core, z = (at_ref[i] for i in range(4))
    tokens = d0.shape[1]
    cols = w_ref.shape[1]
    half = tokens // 2
    order = own_first(core, z, tokens)
    for k, d in enumerate((d0, d1, d2, d3)):
        rel = lax.rem(y + k - x + 4, 4)
        dy_ref[pl.ds(pl.multiple_of(rel * tokens, tokens), tokens), :] = lax.dot_general(
            order, d[...], (((1,), (1,)), ((), ())), preferred_element_type=F32
        ).astype(BF)
    steps = 4
    tile = cols // steps
    for j in range(steps):
        span = pl.ds(j * tile, tile)
        total = jnp.dot(dy_ref[...], w_ref[:, span], preferred_element_type=F32).astype(BF)
        for p in range(4):
            first = p * tokens
            keep_ref[p, :, span] = total[first : first + half]
            send_ref[p, :, span] = total[first + half : first + tokens]


def dgrad(at, blocks, masked):
    hidden, tokens = blocks[0].shape
    cols = masked.shape[1]
    half = shaped(4, tokens // 2, cols)
    return pl.pallas_call(
        dgrad_kernel,
        out_shape=(half, half, shaped(4 * tokens, hidden)),
        in_specs=[SMEM] + [VMEM] * 5,
        out_specs=(VMEM,) * 3,
        cost_estimate=cost(8 * tokens * hidden * cols, 4 << 20),
        compiler_params=grant(12),
        name="dgrad",
    )(at, *blocks, masked)


def fwd_kernel(at_ref, *refs):
    mine, other = refs[:5], refs[5:10]
    w_ref, o0, o1, o2, o3, full_ref, acc_ref = refs[10:]
    x, y = at_ref[0], at_ref[1]
    half = mine[0].shape[0]
    tokens = 2 * half
    for h, group in enumerate((mine, other)):
        for piece, first in zip(group, (0, 2 * half, 4 * half, 4 * half + half // 2, 6 * half)):
            start = first + h * half
            full_ref[start : start + piece.shape[0], :] = piece[...]
    acc_ref[...] = lax.dot_general(
        w_ref[...], full_ref[...], (((1,), (1,)), ((), ())), preferred_element_type=F32
    ).astype(BF)
    for k, out in enumerate((o0, o1, o2, o3)):
        rel = lax.rem(y + k - x + 4, 4)
        out[...] = acc_ref[:, pl.ds(pl.multiple_of(rel * tokens, tokens), tokens)]


def forward(at, mine, other, masked):
    half, cols = mine[0].shape
    hidden = masked.shape[0]
    out = shaped(hidden, 2 * half)
    return pl.pallas_call(
        fwd_kernel,
        out_shape=(out,) * 4 + (shaped(8 * half, cols),),
        in_specs=[SMEM] + [VMEM] * 11,
        out_specs=(VMEM,) * 5,
        scratch_shapes=[pltpu.VMEM((hidden, 8 * half), BF)],
        cost_estimate=cost(16 * half * hidden * cols, 6 << 20),
        compiler_params=grant(14),
        name="forward",
    )(at, *mine, *other, masked)


def wgrad_kernel(dy_ref, a_ref, m_ref, o_hbm, o_ref, sems):
    chunks = sems.shape[0]
    cols = o_ref.shape[1]
    tile = cols // chunks
    rows_b = m_ref.shape[0]
    side = o_ref.shape[0] // rows_b
    left = dy_ref[...].T
    wide = spread(m_ref[...], cols)
    out = []
    for j in range(chunks):
        here = slice(j * tile, (j + 1) * tile)
        total = jnp.dot(left, a_ref[:, here], preferred_element_type=F32)
        for i in range(rows_b):
            span = slice(i * side, (i + 1) * side)
            o_ref[span, here] = (total[span] * wide[i : i + 1, here]).astype(BF)
        part = pl.ds(j * tile, tile)
        out.append(pltpu.make_async_copy(o_ref.at[:, part], o_hbm.at[:, part], sems.at[j]))
        out[-1].start()
    for copy in out:
        copy.wait()


def wgrad(dy, full, mt):
    rows, hidden = dy.shape
    cols = full.shape[1]
    return pl.pallas_call(
        wgrad_kernel,
        out_shape=shaped(hidden, cols),
        in_specs=[VMEM] * 3,
        out_specs=HBM,
        scratch_shapes=[pltpu.VMEM((hidden, cols), BF), pltpu.SemaphoreType.DMA((4,))],
        cost_estimate=cost(2 * rows * hidden * cols, 6 << 20),
        compiler_params=grant(14),
        name="wgrad",
    )(dy, full, mt)


def finish_kernel(at_ref, r0, r1, r2, r3, o_ref):
    total = (r0[...].astype(F32) + r1[...].astype(F32)) + (
        r2[...].astype(F32) + r3[...].astype(F32)
    )
    back = own_first(at_ref[2], at_ref[3], r0.shape[1])
    o_ref[...] = jnp.dot(total.astype(BF), back, preferred_element_type=F32).astype(BF)


def finish(at, parts):
    return pl.pallas_call(
        finish_kernel,
        out_shape=shaped(*parts[0].shape),
        in_specs=[SMEM] + [VMEM] * 4,
        out_specs=VMEM,
        cost_estimate=cost(parts[0].size * 256, 1 << 20),
        compiler_params=grant(6),
        name="finish",
    )(at, *parts)


def to(array, axis, step):
    n = lax.axis_size(axis)
    return lax.ppermute(array, axis, [(i, (i + step) % n) for i in range(n)])


def across(array, step):
    n = lax.axis_size("z")
    return lax.ppermute(array, "z", [(i, (i - step if i % 2 else i + step) % n) for i in range(n)])


def with_partner(array, step):
    return jnp.concatenate([array, across(array, step)])


def halved(*terms):
    half = terms[0].shape[0] // 2
    return added(*(t[:half] for t in terms)), added(*(t[half:] for t in terms))


def added(*terms):
    return sum(t.astype(F32) for t in terms).astype(BF)


def on_device(activations, up_weight, block_mask, out_grad):
    at = jnp.stack([lax.axis_index(n).astype(jnp.int32) for n in ("x", "narrow", "core", "z")])
    wt, mt, dyt = up_weight.T, block_mask.T, out_grad.T

    blocks = (dyt, to(dyt, "narrow", -1), to(dyt, "narrow", 2), to(dyt, "narrow", 1))
    masked = masked_weight(in_hbm(mt), in_hbm(wt))
    near = with_partner(activations, STEPS[0])
    keep, send, dy = dgrad(at, blocks, masked)
    got = to(send, "core", 1)
    near = with_partner(near, STEPS[1])
    near = with_partner(near, STEPS[2])
    half = keep.shape[1] // 2
    low, high = halved(keep[2], got[2])
    ahead = to(low, "x", 1)
    behind = to(high, "x", -1)
    none = jnp.zeros_like(ahead)
    right = added(keep[1], got[1], jnp.concatenate([ahead, none]))
    left = added(keep[3], got[3], jnp.concatenate([none, behind]))
    right = to(right, "x", 1)
    left = to(left, "x", -1)
    own, away = halved(keep[0], got[0], right, left)
    came = across(away, STEPS[2])
    own, away = halved(own, came)
    came = across(away, STEPS[1])
    own, away = halved(own, came)
    came = across(away, STEPS[0])
    input_grad = added(own, came)

    before = to(near, "x", 1)
    after = to(near, "x", -1)
    far_low = to(before[:half], "x", 1)
    far_high = to(after[half:], "x", -1)
    mine = (near, after, far_low, far_high, before)
    near, after, before = (to(m, "core", 1) for m in (near, after, before))
    far_low, far_high = to(far_low, "core", 1), to(far_high, "core", 1)
    other = (near, after, far_low, far_high, before)
    o0, o1, o2, o3, full = forward(at, mine, other, masked)
    parts = (o0, to(o1, "narrow", 1), to(o2, "narrow", 2), to(o3, "narrow", -1))
    output = finish(at, parts).T
    weight_grad = wgrad(dy, full, mt).T
    return (output, input_grad, weight_grad)


def solution(mesh):
    torus = Mesh(
        mesh.devices.reshape(4, 8, 2, mesh.shape["narrow"]),
        ("x", "z", "core", "narrow"),
    )
    return jax.shard_map(
        on_device,
        mesh=torus,
        in_specs=(P(WIDE, "narrow"), P("narrow", WIDE), P("narrow", WIDE), P("narrow", WIDE)),
        out_specs=(P("narrow", WIDE), P(WIDE, "narrow"), P("narrow", WIDE)),
        check_vma=False,
    )
```

```python
import jax
import jax.numpy as jnp
from jax import lax
from jax.experimental import pallas as pl
from jax.experimental.pallas import tpu as pltpu
from jax.sharding import Mesh
from jax.sharding import PartitionSpec as P

WIDE = ("x", "z", "core")
STEPS = (3, -1, 1)
BF = jnp.bfloat16
F32 = jnp.float32
VMEM = pl.BlockSpec(memory_space=pltpu.VMEM)
HBM = pl.BlockSpec(memory_space=pltpu.HBM)
SMEM = pl.BlockSpec(memory_space=pltpu.SMEM)


def cost(flops, moved):
    return pl.CostEstimate(flops=flops, bytes_accessed=moved, transcendentals=0)


def grant(mib):
    return pltpu.CompilerParams(vmem_limit_bytes=mib << 20)


def in_hbm(array):
    return pltpu.with_memory_space_constraint(array, pltpu.HBM)


def shaped(*dims, kind=BF):
    return jax.ShapeDtypeStruct(dims, kind)


def spread(mask, cols):
    cols_b = mask.shape[1]
    side = cols // cols_b
    block = lax.broadcasted_iota(jnp.int32, (cols_b, cols), 0)
    at = lax.broadcasted_iota(jnp.int32, (cols_b, cols), 1)
    first = block * side
    pick = jnp.logical_and(at >= first, at < first + side).astype(F32)
    return jnp.dot(mask.astype(F32), pick, preferred_element_type=F32)


def own_first(core, z, tokens):
    new = lax.broadcasted_iota(jnp.int32, (tokens, tokens), 0)
    old = lax.broadcasted_iota(jnp.int32, (tokens, tokens), 1)
    half = tokens // 2
    other = (new >= half).astype(jnp.int32)
    within = new - other * half
    group = jnp.right_shift(within, 3)
    row = within - group * 8
    at = jnp.zeros_like(group) + z
    for bit, step in zip((2, 1, 0), reversed(STEPS)):
        moved = jnp.bitwise_and(jnp.right_shift(group, bit), 1) * step
        at = at + moved * (1 - 2 * jnp.bitwise_and(at, 1))
    src = jnp.bitwise_and(at, 7) * 16 + jnp.bitwise_xor(other, core) * 8 + row
    return (src == old).astype(BF)


def mask_kernel(m_hbm, w_hbm, masked_ref, m_ref, w_ref, m_sem, sems):
    rows, cols = w_ref.shape
    rows_b = m_ref.shape[0]
    side = rows // rows_b
    spans = [pl.ds(i * side, side) for i in range(rows_b)]
    first = pltpu.make_async_copy(m_hbm, m_ref, m_sem)
    first.start()
    loads = [
        pltpu.make_async_copy(w_hbm.at[span], w_ref.at[span], sems.at[i])
        for i, span in enumerate(spans)
    ]
    for load in loads:
        load.start()
    first.wait()
    wide = spread(m_ref[...], cols)
    for i, span in enumerate(spans):
        loads[i].wait()
        masked_ref[span, :] = w_ref[span, :] * wide[i : i + 1, :].astype(BF)


def masked_weight(mt, wt):
    hidden, cols = wt.shape
    return pl.pallas_call(
        mask_kernel,
        out_shape=shaped(hidden, cols),
        in_specs=[HBM, HBM],
        out_specs=VMEM,
        scratch_shapes=[
            pltpu.VMEM(mt.shape, jnp.int32),
            pltpu.VMEM((hidden, cols), BF),
            pltpu.SemaphoreType.DMA,
            pltpu.SemaphoreType.DMA((mt.shape[0],)),
        ],
        cost_estimate=cost(2 * hidden * cols, 4 << 20),
        compiler_params=grant(10),
        name="mask_weight",
    )(mt, wt)


def dgrad_kernel(at_ref, d0, d1, d2, d3, w_ref, keep_ref, far_ref, send_ref, dy_ref):
    x, y, core, z = (at_ref[i] for i in range(4))
    tokens = d0.shape[1]
    cols = w_ref.shape[1]
    half = tokens // 2
    order = own_first(core, z, tokens)
    for k, d in enumerate((d0, d1, d2, d3)):
        rel = lax.rem(y + k - x + 4, 4)
        dy_ref[pl.ds(pl.multiple_of(rel * tokens, tokens), tokens), :] = lax.dot_general(
            order, d[...], (((1,), (1,)), ((), ())), preferred_element_type=F32
        ).astype(BF)
    steps = 4
    tile = cols // steps
    for j in range(steps):
        span = pl.ds(j * tile, tile)
        total = jnp.dot(dy_ref[...], w_ref[:, span], preferred_element_type=F32).astype(BF)
        for p in range(4):
            first = p * tokens
            keep_ref[p, :, span] = total[first : first + half]
            other = total[first + half : first + tokens]
            if p == 2:
                far_ref[:, span] = other
            else:
                send_ref[min(p, 2), :, span] = other


def dgrad(at, blocks, masked):
    hidden, tokens = blocks[0].shape
    cols = masked.shape[1]
    half = tokens // 2
    return pl.pallas_call(
        dgrad_kernel,
        out_shape=(
            shaped(4, half, cols),
            shaped(half, cols),
            shaped(3, half, cols),
            shaped(4 * tokens, hidden),
        ),
        in_specs=[SMEM] + [VMEM] * 5,
        out_specs=(VMEM,) * 4,
        cost_estimate=cost(8 * tokens * hidden * cols, 4 << 20),
        compiler_params=grant(12),
        name="dgrad",
    )(at, *blocks, masked)


def join_kernel(*refs):
    rows = refs[0].shape[0]
    for i, ref in enumerate(refs[:-1]):
        refs[-1][i * rows : (i + 1) * rows, :] = ref[...]


def join(parts):
    rows, cols = parts[0].shape
    return pl.pallas_call(
        join_kernel,
        out_shape=shaped(len(parts) * rows, cols),
        in_specs=[VMEM] * len(parts),
        out_specs=VMEM,
        cost_estimate=cost(0, 4 * len(parts) * rows * cols),
        compiler_params=grant(4),
        name="join",
    )(*parts)


def fwd_kernel(at_ref, *refs):
    pieces = refs[:8]
    w_ref, o0, o1, o2, o3, full_ref, acc_ref = refs[8:]
    x, y = at_ref[0], at_ref[1]
    rows = pieces[0].shape[0] // 4
    tokens = 8 * rows
    for i, piece in enumerate(pieces):
        for p in range(4):
            start = p * tokens + i * rows
            full_ref[start : start + rows, :] = piece[p * rows : (p + 1) * rows, :]
    acc_ref[...] = lax.dot_general(
        w_ref[...], full_ref[...], (((1,), (1,)), ((), ())), preferred_element_type=F32
    ).astype(BF)
    for k, out in enumerate((o0, o1, o2, o3)):
        rel = lax.rem(y + k - x + 4, 4)
        out[...] = acc_ref[:, pl.ds(pl.multiple_of(rel * tokens, tokens), tokens)]


def forward(at, pieces, masked):
    rows, cols = pieces[0].shape
    hidden = masked.shape[0]
    out = shaped(hidden, 2 * rows)
    return pl.pallas_call(
        fwd_kernel,
        out_shape=(out,) * 4 + (shaped(8 * rows, cols),),
        in_specs=[SMEM] + [VMEM] * 9,
        out_specs=(VMEM,) * 5,
        scratch_shapes=[pltpu.VMEM((hidden, 8 * rows), BF)],
        cost_estimate=cost(16 * rows * hidden * cols, 6 << 20),
        compiler_params=grant(14),
        name="forward",
    )(at, *pieces, masked)


def wgrad_kernel(dy_ref, a_ref, m_ref, o_hbm, o_ref, sems):
    chunks = sems.shape[0]
    cols = o_ref.shape[1]
    tile = cols // chunks
    rows_b = m_ref.shape[0]
    side = o_ref.shape[0] // rows_b
    left = dy_ref[...].T
    wide = spread(m_ref[...], cols)
    out = []
    for j in range(chunks):
        here = slice(j * tile, (j + 1) * tile)
        total = jnp.dot(left, a_ref[:, here], preferred_element_type=F32)
        for i in range(rows_b):
            span = slice(i * side, (i + 1) * side)
            o_ref[span, here] = (total[span] * wide[i : i + 1, here]).astype(BF)
        part = pl.ds(j * tile, tile)
        out.append(pltpu.make_async_copy(o_ref.at[:, part], o_hbm.at[:, part], sems.at[j]))
        out[-1].start()
    for copy in out:
        copy.wait()


def wgrad(dy, full, mt):
    rows, hidden = dy.shape
    cols = full.shape[1]
    return pl.pallas_call(
        wgrad_kernel,
        out_shape=shaped(hidden, cols),
        in_specs=[VMEM] * 3,
        out_specs=HBM,
        scratch_shapes=[pltpu.VMEM((hidden, cols), BF), pltpu.SemaphoreType.DMA((4,))],
        cost_estimate=cost(2 * rows * hidden * cols, 6 << 20),
        compiler_params=grant(14),
        name="wgrad",
    )(dy, full, mt)


def finish_kernel(at_ref, r0, r1, r2, r3, o_ref):
    total = (r0[...].astype(F32) + r1[...].astype(F32)) + (
        r2[...].astype(F32) + r3[...].astype(F32)
    )
    back = own_first(at_ref[2], at_ref[3], r0.shape[1])
    o_ref[...] = jnp.dot(total.astype(BF), back, preferred_element_type=F32).astype(BF)


def finish(at, parts):
    return pl.pallas_call(
        finish_kernel,
        out_shape=shaped(*parts[0].shape),
        in_specs=[SMEM] + [VMEM] * 4,
        out_specs=VMEM,
        cost_estimate=cost(parts[0].size * 256, 1 << 20),
        compiler_params=grant(6),
        name="finish",
    )(at, *parts)


def to(array, axis, step):
    n = lax.axis_size(axis)
    return lax.ppermute(array, axis, [(i, (i + step) % n) for i in range(n)])


def across(array, step):
    n = lax.axis_size("z")
    return lax.ppermute(array, "z", [(i, (i - step if i % 2 else i + step) % n) for i in range(n)])


def with_partner(array, step):
    return join((array, across(array, step)))


def halved(*terms):
    half = terms[0].shape[0] // 2
    return added(*(t[:half] for t in terms)), added(*(t[half:] for t in terms))


def added(*terms):
    return sum(t.astype(F32) for t in terms).astype(BF)


def on_device(activations, up_weight, block_mask, out_grad):
    at = jnp.stack([lax.axis_index(n).astype(jnp.int32) for n in ("x", "narrow", "core", "z")])
    wt, mt, dyt = up_weight.T, block_mask.T, out_grad.T

    blocks = (dyt, to(dyt, "narrow", -1), to(dyt, "narrow", 2), to(dyt, "narrow", 1))
    near = with_partner(activations, STEPS[0])
    far = to(near, "x", 2)
    before, after = to(near, "x", 1), to(near, "x", -1)
    masked = masked_weight(in_hbm(mt), in_hbm(wt))
    keep, send_far, send, dy = dgrad(at, blocks, masked)
    got_far = to(send_far, "core", 1)
    got = to(send, "core", 1)
    own = join((near, after, far, before))
    side = across(own, STEPS[1])
    up_own = across(own, STEPS[2])
    up_side = across(side, STEPS[2])
    pieces = own, side, up_own, up_side
    swapped = [to(piece, "core", 1) for piece in pieces[:3]]
    swapped.append(to(up_side, "core", 1))
    low, high = halved(keep[2], got_far)
    ahead = to(low, "x", 1)
    behind = to(high, "x", -1)
    none = jnp.zeros_like(ahead)
    right = added(keep[1], got[1], jnp.concatenate([ahead, none]))
    left = added(keep[3], got[2], jnp.concatenate([none, behind]))
    right = to(right, "x", 1)
    left = to(left, "x", -1)
    rest, away = halved(keep[0], got[0], right, left)
    came = across(away, STEPS[2])
    rest, away = halved(rest, came)
    came = across(away, STEPS[1])
    rest, away = halved(rest, came)
    came = across(away, STEPS[0])
    input_grad = added(rest, came)

    o0, o1, o2, o3, full = forward(at, (*pieces, *swapped), masked)
    parts = (o0, to(o1, "narrow", 1), to(o2, "narrow", 2), to(o3, "narrow", -1))
    output = finish(at, parts).T
    weight_grad = wgrad(dy, full, mt).T
    return (output, input_grad, weight_grad)


def solution(mesh):
    torus = Mesh(
        mesh.devices.reshape(4, 8, 2, mesh.shape["narrow"]),
        ("x", "z", "core", "narrow"),
    )
    return jax.shard_map(
        on_device,
        mesh=torus,
        in_specs=(P(WIDE, "narrow"), P("narrow", WIDE), P("narrow", WIDE), P("narrow", WIDE)),
        out_specs=(P("narrow", WIDE), P(WIDE, "narrow"), P("narrow", WIDE)),
        check_vma=False,
    )
```

```python
import jax
import jax.numpy as jnp
from jax import lax
from jax.experimental import pallas as pl
from jax.experimental.pallas import tpu as pltpu
from jax.sharding import Mesh
from jax.sharding import PartitionSpec as P

WIDE = ("x", "z", "core")
STEPS = (3, -1, 1)
BF = jnp.bfloat16
F32 = jnp.float32
VMEM = pl.BlockSpec(memory_space=pltpu.VMEM)
HBM = pl.BlockSpec(memory_space=pltpu.HBM)
SMEM = pl.BlockSpec(memory_space=pltpu.SMEM)


def cost(flops, moved):
    return pl.CostEstimate(flops=flops, bytes_accessed=moved, transcendentals=0)


def grant(mib):
    return pltpu.CompilerParams(vmem_limit_bytes=mib << 20)


def in_hbm(array):
    return pltpu.with_memory_space_constraint(array, pltpu.HBM)


def shaped(*dims, kind=BF):
    return jax.ShapeDtypeStruct(dims, kind)


def spread(mask, cols):
    cols_b = mask.shape[1]
    side = cols // cols_b
    block = lax.broadcasted_iota(jnp.int32, (cols_b, cols), 0)
    at = lax.broadcasted_iota(jnp.int32, (cols_b, cols), 1)
    first = block * side
    pick = jnp.logical_and(at >= first, at < first + side).astype(F32)
    return jnp.dot(mask.astype(F32), pick, preferred_element_type=F32)


def own_first(core, z, tokens):
    new = lax.broadcasted_iota(jnp.int32, (tokens, tokens), 0)
    old = lax.broadcasted_iota(jnp.int32, (tokens, tokens), 1)
    half = tokens // 2
    other = (new >= half).astype(jnp.int32)
    within = new - other * half
    group = jnp.right_shift(within, 3)
    row = within - group * 8
    at = jnp.zeros_like(group) + z
    for bit, step in zip((2, 1, 0), reversed(STEPS)):
        moved = jnp.bitwise_and(jnp.right_shift(group, bit), 1) * step
        at = at + moved * (1 - 2 * jnp.bitwise_and(at, 1))
    src = jnp.bitwise_and(at, 7) * 16 + jnp.bitwise_xor(other, core) * 8 + row
    return (src == old).astype(BF)


def mask_kernel(m_hbm, w_hbm, masked_ref, m_ref, w_ref, m_sem, sems):
    rows, cols = w_ref.shape
    rows_b = m_ref.shape[0]
    side = rows // rows_b
    spans = [pl.ds(i * side, side) for i in range(rows_b)]
    first = pltpu.make_async_copy(m_hbm, m_ref, m_sem)
    first.start()
    loads = [
        pltpu.make_async_copy(w_hbm.at[span], w_ref.at[span], sems.at[i])
        for i, span in enumerate(spans)
    ]
    for load in loads:
        load.start()
    first.wait()
    wide = spread(m_ref[...], cols)
    for i, span in enumerate(spans):
        loads[i].wait()
        masked_ref[span, :] = w_ref[span, :] * wide[i : i + 1, :].astype(BF)


def masked_weight(mt, wt):
    hidden, cols = wt.shape
    return pl.pallas_call(
        mask_kernel,
        out_shape=shaped(hidden, cols),
        in_specs=[HBM, HBM],
        out_specs=VMEM,
        scratch_shapes=[
            pltpu.VMEM(mt.shape, jnp.int32),
            pltpu.VMEM((hidden, cols), BF),
            pltpu.SemaphoreType.DMA,
            pltpu.SemaphoreType.DMA((mt.shape[0],)),
        ],
        cost_estimate=cost(2 * hidden * cols, 4 << 20),
        compiler_params=grant(10),
        name="mask_weight",
    )(mt, wt)


def dgrad_kernel(at_ref, d0, d1, d2, d3, w_ref, keep_ref, far_ref, send_ref, dy_ref):
    x, y, core, z = (at_ref[i] for i in range(4))
    tokens = d0.shape[1]
    cols = w_ref.shape[1]
    half = tokens // 2
    order = own_first(core, z, tokens)
    for k, d in enumerate((d0, d1, d2, d3)):
        rel = lax.rem(y + k - x + 4, 4)
        dy_ref[pl.ds(pl.multiple_of(rel * tokens, tokens), tokens), :] = lax.dot_general(
            order, d[...], (((1,), (1,)), ((), ())), preferred_element_type=F32
        ).astype(BF)
    steps = 4
    tile = cols // steps
    for j in range(steps):
        span = pl.ds(j * tile, tile)
        total = jnp.dot(dy_ref[...], w_ref[:, span], preferred_element_type=F32).astype(BF)
        for p in range(4):
            first = p * tokens
            keep_ref[p, :, span] = total[first : first + half]
            other = total[first + half : first + tokens]
            if p == 2:
                far_ref[:, span] = other
            else:
                send_ref[min(p, 2), :, span] = other


def dgrad(at, blocks, masked):
    hidden, tokens = blocks[0].shape
    cols = masked.shape[1]
    half = tokens // 2
    return pl.pallas_call(
        dgrad_kernel,
        out_shape=(
            shaped(4, half, cols),
            shaped(half, cols),
            shaped(3, half, cols),
            shaped(4 * tokens, hidden),
        ),
        in_specs=[SMEM] + [VMEM] * 5,
        out_specs=(VMEM,) * 4,
        cost_estimate=cost(8 * tokens * hidden * cols, 4 << 20),
        compiler_params=grant(12),
        name="dgrad",
    )(at, *blocks, masked)


def join_kernel(*refs):
    rows = refs[0].shape[0]
    for i, ref in enumerate(refs[:-1]):
        refs[-1][i * rows : (i + 1) * rows, :] = ref[...]


def join(parts):
    rows, cols = parts[0].shape
    return pl.pallas_call(
        join_kernel,
        out_shape=shaped(len(parts) * rows, cols),
        in_specs=[VMEM] * len(parts),
        out_specs=VMEM,
        cost_estimate=cost(0, 4 * len(parts) * rows * cols),
        compiler_params=grant(4),
        name="join",
    )(*parts)


def fwd_kernel(at_ref, *refs):
    pieces = refs[:8]
    w_ref, o0, o1, o2, o3, full_ref, acc_ref = refs[8:]
    x, y = at_ref[0], at_ref[1]
    rows = pieces[0].shape[0] // 4
    tokens = 8 * rows
    for i, piece in enumerate(pieces):
        for p in range(4):
            start = p * tokens + i * rows
            full_ref[start : start + rows, :] = piece[p * rows : (p + 1) * rows, :]
    acc_ref[...] = lax.dot_general(
        w_ref[...], full_ref[...], (((1,), (1,)), ((), ())), preferred_element_type=F32
    ).astype(BF)
    for k, out in enumerate((o0, o1, o2, o3)):
        rel = lax.rem(y + k - x + 4, 4)
        out[...] = acc_ref[:, pl.ds(pl.multiple_of(rel * tokens, tokens), tokens)]


def forward(at, pieces, masked):
    rows, cols = pieces[0].shape
    hidden = masked.shape[0]
    out = shaped(hidden, 2 * rows)
    return pl.pallas_call(
        fwd_kernel,
        out_shape=(out,) * 4 + (shaped(8 * rows, cols),),
        in_specs=[SMEM] + [VMEM] * 9,
        out_specs=(VMEM,) * 5,
        scratch_shapes=[pltpu.VMEM((hidden, 8 * rows), BF)],
        cost_estimate=cost(16 * rows * hidden * cols, 6 << 20),
        compiler_params=grant(14),
        name="forward",
    )(at, *pieces, masked)


def wgrad_kernel(dy_ref, a_ref, m_ref, o_hbm, o_ref, sems):
    chunks = sems.shape[0]
    cols = o_ref.shape[1]
    tile = cols // chunks
    rows_b = m_ref.shape[0]
    side = o_ref.shape[0] // rows_b
    left = dy_ref[...].T
    wide = spread(m_ref[...], cols)
    out = []
    for j in range(chunks):
        here = slice(j * tile, (j + 1) * tile)
        total = jnp.dot(left, a_ref[:, here], preferred_element_type=F32)
        for i in range(rows_b):
            span = slice(i * side, (i + 1) * side)
            o_ref[span, here] = (total[span] * wide[i : i + 1, here]).astype(BF)
        part = pl.ds(j * tile, tile)
        out.append(pltpu.make_async_copy(o_ref.at[:, part], o_hbm.at[:, part], sems.at[j]))
        out[-1].start()
    for copy in out:
        copy.wait()


def wgrad(dy, full, mt):
    rows, hidden = dy.shape
    cols = full.shape[1]
    return pl.pallas_call(
        wgrad_kernel,
        out_shape=shaped(hidden, cols),
        in_specs=[VMEM] * 3,
        out_specs=HBM,
        scratch_shapes=[pltpu.VMEM((hidden, cols), BF), pltpu.SemaphoreType.DMA((4,))],
        cost_estimate=cost(2 * rows * hidden * cols, 6 << 20),
        compiler_params=grant(14),
        name="wgrad",
    )(dy, full, mt)


def finish_kernel(at_ref, r0, r1, r2, r3, o_ref):
    total = (r0[...].astype(F32) + r1[...].astype(F32)) + (
        r2[...].astype(F32) + r3[...].astype(F32)
    )
    back = own_first(at_ref[2], at_ref[3], r0.shape[1])
    o_ref[...] = jnp.dot(total.astype(BF), back, preferred_element_type=F32).astype(BF)


def finish(at, parts):
    return pl.pallas_call(
        finish_kernel,
        out_shape=shaped(*parts[0].shape),
        in_specs=[SMEM] + [VMEM] * 4,
        out_specs=VMEM,
        cost_estimate=cost(parts[0].size * 256, 1 << 20),
        compiler_params=grant(6),
        name="finish",
    )(at, *parts)


def to(array, axis, step):
    n = lax.axis_size(axis)
    return lax.ppermute(array, axis, [(i, (i + step) % n) for i in range(n)])


def across(array, step):
    n = lax.axis_size("z")
    return lax.ppermute(array, "z", [(i, (i - step if i % 2 else i + step) % n) for i in range(n)])


def with_partner(array, step):
    return join((array, across(array, step)))


def halved(*terms):
    half = terms[0].shape[0] // 2
    return added(*(t[:half] for t in terms)), added(*(t[half:] for t in terms))


def added(*terms):
    return sum(t.astype(F32) for t in terms).astype(BF)


def on_device(activations, up_weight, block_mask, out_grad):
    at = jnp.stack([lax.axis_index(n).astype(jnp.int32) for n in ("x", "narrow", "core", "z")])
    wt, mt, dyt = up_weight.T, block_mask.T, out_grad.T

    blocks = (dyt, to(dyt, "narrow", -1), to(dyt, "narrow", 2), to(dyt, "narrow", 1))
    near = with_partner(activations, STEPS[0])
    far = to(near, "x", 2)
    before, after = to(near, "x", 1), to(near, "x", -1)
    masked = masked_weight(in_hbm(mt), in_hbm(wt))
    keep, send_far, send, dy = dgrad(at, blocks, masked)
    got_far = to(send_far, "core", 1)
    got = to(send, "core", 1)
    own = join((near, after, far, before))
    side = across(own, STEPS[1])
    up_own = across(own, STEPS[2])
    up_side = across(side, STEPS[2])
    pieces = own, side, up_own, up_side
    swapped = [to(own, "core", 1)]
    swapped += [to(piece, "core", 1) for piece in pieces[1:3]]
    swapped.append(to(up_side, "core", 1))
    second = added(keep[2], got_far)
    behind = to(second, "x", -1)
    first = added(keep[1], got[1])
    direct = to(first, "x", 1)
    third = added(keep[3], got[2], behind)
    relayed = to(third, "x", -1)
    rest, away = halved(keep[0], got[0], direct, relayed)
    came = across(away, STEPS[2])
    rest, away = halved(rest, came)
    came = across(away, STEPS[1])
    rest, away = halved(rest, came)
    came = across(away, STEPS[0])
    input_grad = added(rest, came)

    o0, o1, o2, o3, full = forward(at, (*pieces, *swapped), masked)
    far_out = to(o2, "narrow", 2)
    parts = (o0, to(o1, "narrow", 1), far_out, to(o3, "narrow", -1))
    output = finish(at, parts).T
    weight_grad = wgrad(dy, full, mt).T
    return (output, input_grad, weight_grad)


def solution(mesh):
    torus = Mesh(
        mesh.devices.reshape(4, 8, 2, mesh.shape["narrow"]),
        ("x", "z", "core", "narrow"),
    )
    return jax.shard_map(
        on_device,
        mesh=torus,
        in_specs=(P(WIDE, "narrow"), P("narrow", WIDE), P("narrow", WIDE), P("narrow", WIDE)),
        out_specs=(P("narrow", WIDE), P(WIDE, "narrow"), P("narrow", WIDE)),
        check_vma=False,
    )
```
